256 devices in a mesh: dp: 8 (over y, x_lo), tensor: 32 (over z, x_hi, core).
Axes of the slice: x: 4 (x_hi: 2, x_lo: 2; x = x_hi * 2 + x_lo), y: 4, z: 8, core: 2. Of those that a mesh axis runs over, the one named last changes fastest.
Arguments:
- tokens: bfloat16 [2048, 3072], P('dp', 'tensor'), may hold values from -6 to 6
- buckets: int32 [2048], P('dp'), may hold values from 0 to 999
- modulation: float32 [1000, 3, 3072], P(None, None, 'tensor'), may hold values from -3 to 3
- up_weight: bfloat16 [3072, 12288], P(None, 'tensor'), may hold values from -0.109375 to 0.109375
- down_weight: bfloat16 [3072, 12288], P(None, 'tensor'), may hold values from -0.0546875 to 0.0546875
- output_cotangent: bfloat16 [2048, 3072], P('dp', 'tensor'), may hold values from -6 to 6
Outputs:
- mixed: bfloat16 [2048, 3072], P('dp', 'tensor')
- token_input_gradient: bfloat16 [2048, 3072], P('dp', 'tensor')
- grad_up: float32 [3072, 12288], P('dp', 'tensor')
- grad_down: float32 [3072, 12288], P('dp', 'tensor')
The draws below stay inside these ranges and needn't reach their ends.
All inputs are finite; a program needn't handle non-finite values.
Results may differ from the reference program's by a relative error of at most 0.0062.
Values may be sent and summed in bfloat16 or wider, within the bound.
A program may use at most 64 MiB of HBM per device.

```python
import jax
import jax.numpy as jnp
from jax import lax

D = 3072
FF = 12288
BUCKETS = 1000
TOKENS = 2048


def with_ends(values, own_key, least, top_value):
    longest = values.shape.index(max(values.shape))
    spots = []
    for shift in (0, 1):
        where = [jax.random.randint(jax.random.fold_in(own_key, axis), (), 0, length) for axis, length in enumerate(values.shape)]
        where[longest] = (where[longest] + shift) % values.shape[longest]
        spots.append(tuple(where))
    return values.at[spots[0]].set(least).at[spots[1]].set(top_value)


def shard_levels(key, dims, cuts, low, high):
    factor_of, own = 1.0, jax.random.fold_in(key, 6)
    for position, blocks in cuts:
        draws = jnp.exp(jax.random.uniform(jax.random.fold_in(own, position), (blocks,), jnp.float32, low / len(cuts), high / len(cuts)))
        factor_of = factor_of * jnp.repeat(draws, dims[position] // blocks).reshape([-1 if axis == position else 1 for axis in range(len(dims))])
    return factor_of


def gaussian(stream_key, dims, width, limit, cuts=(), kind=jnp.bfloat16):
    gain = shard_levels(stream_key, dims, cuts, -0.22, 0.18) if cuts else 1.0
    entries = jax.random.normal(stream_key, dims, jnp.float32) * width * gain
    return jnp.minimum(jnp.maximum(entries, -limit), limit).astype(kind)


def setup_inputs(seed: int = 0) -> dict:
    splits = jax.random.split(jax.random.key(seed), 7)
    return {
        "tokens": gaussian(splits[0], (TOKENS, D), 1.0, 6.0, ((0, 8), (1, 32))),
        "buckets": with_ends(jax.random.randint(splits[1], (TOKENS,), 0, BUCKETS), jax.random.fold_in(splits[1], 1), 0, BUCKETS - 1).astype(jnp.int32),
        "modulation": gaussian(splits[2], (BUCKETS, 3, D), 0.5, 3.0, ((2, 32),), jnp.float32),
        "up_weight": gaussian(splits[3], (D, FF), D ** -0.5, 0.109375, ((1, 32),)),
        "down_weight": gaussian(splits[4], (D, FF), FF ** -0.5, 0.0546875, ((1, 32),)),
        "output_cotangent": gaussian(splits[5], (TOKENS, D), 1.0, 6.0, ((0, 8), (1, 32))),
    }


def gelu_tanh(value):
    return jax.nn.gelu(value, approximate=True)

def reference(tokens, buckets, modulation, up_weight, down_weight, output_cotangent):
    model_width = tokens.shape[1]
    input_tokens = tokens.astype(jnp.float32)
    cond = jnp.take(modulation, buckets, axis=0)
    modulation_shift = cond[:, 0]
    modulation_scale = cond[:, 1]
    gate = cond[:, 2]
    row_mean = lax.optimization_barrier(jnp.sum(input_tokens, axis=1)) / model_width
    var = lax.optimization_barrier(jnp.sum(input_tokens * input_tokens, axis=1)) / model_width - row_mean * row_mean
    inverse_deviation = lax.rsqrt(var + 1e-06)
    normalized_input = (input_tokens - row_mean[:, None]) * inverse_deviation[:, None]
    hidden_input_rows = (normalized_input * (1.0 + modulation_scale) + modulation_shift).astype(jnp.bfloat16)
    pre = jnp.dot(hidden_input_rows, up_weight, preferred_element_type=jnp.float32)
    act = gelu_tanh(pre).astype(jnp.bfloat16)
    velocity = jnp.dot(act, down_weight.T, preferred_element_type=jnp.float32)
    mixed = (input_tokens + gate * velocity).astype(jnp.bfloat16)
    dvel = (output_cotangent.astype(jnp.float32) * gate).astype(jnp.bfloat16)
    dact = jnp.dot(dvel, down_weight, preferred_element_type=jnp.float32)
    pull = jax.vjp(gelu_tanh, pre)[1]
    dpre = pull(dact)[0].astype(jnp.bfloat16)
    grad_down = jnp.dot(dvel.T, act, preferred_element_type=jnp.float32)
    grad_up = jnp.dot(hidden_input_rows.T, dpre, preferred_element_type=jnp.float32)
    dh = jnp.dot(dpre, up_weight.T, preferred_element_type=jnp.float32)
    normalized_input_gradient = dh * (1.0 + modulation_scale)
    first_product = lax.optimization_barrier(jnp.sum(normalized_input_gradient, axis=1)) / model_width
    second_product = lax.optimization_barrier(jnp.sum(normalized_input_gradient * normalized_input, axis=1)) / model_width
    token_input_gradient = output_cotangent.astype(jnp.float32) + inverse_deviation[:, None] * (normalized_input_gradient - first_product[:, None] - normalized_input * second_product[:, None])
    return (mixed, token_input_gradient.astype(jnp.bfloat16), grad_up, grad_down)
```

```python
import functools

import jax
import jax.numpy as jnp
from jax import lax
from jax.experimental import pallas as pl
from jax.experimental.pallas import tpu as pltpu
from jax.sharding import PartitionSpec as P

MESH = pl.DeviceIdType.MESH
BF = jnp.bfloat16
F32 = jnp.float32
NT = (((1,), (1,)), ((), ()))
ORDER = (4, 3, -3, 2, -2, 1, -1, 0)
N_COPIES = 136


def hops(lane, way):
    return 4 if (lane == 0) == (way == 1) else 3


def dot(a, b):
    return jnp.dot(a, b, preferred_element_type=F32)


def block_kernel(
    width,
    x_ref,
    cot_ref,
    mod_ref,
    down_hbm,
    up_hbm,
    mixed_ref,
    tok_ref,
    gd_ref,
    gu_ref,
    W,
    WT,
    G,
    GP,
    ST,
    SZ,
    XH,
    DA,
    AD,
    ADP,
    VS,
    R1,
    PT,
    SB,
    RB,
    XS,
    XR,
    GS,
    GR,
    send_sem,
    recv_sem,
    w_sem,
):
    d, t = lax.axis_index("dp"), lax.axis_index("tensor")
    z, xh, c = t // 4, (t // 2) % 2, t % 2
    y, xl = d // 2, d % 2
    rows, tokens = x_ref.shape
    hidden = W.shape[-1]

    def at(zz, hi, core):
        return (d, zz * 4 + hi * 2 + core)

    def zoff(off):
        return lax.rem(z + off % 8, 8)

    sibling = at(z, xh, 1 - c)
    xpart = at(z, 1 - xh, c)
    xcross = at(z, 1 - xh, 1 - c)
    zpeers = [at(zoff(k), xh, c) for k in range(1, 8)]
    xlo = (y * 2 + 1 - xl, t)
    ypeers = [(lax.rem(y + j, 4) * 2 + xl, t) for j in range(1, 4)]
    local = [sibling, xpart, xcross]

    flight = {}

    def send(key, src, dst, device):
        n = len(flight)
        copy = pltpu.make_async_remote_copy(
            src_ref=src,
            dst_ref=dst,
            send_sem=send_sem.at[n],
            recv_sem=recv_sem.at[n],
            device_id=device,
            device_id_type=MESH,
        )
        copy.start()
        flight[key] = copy

    def arrived(*key):
        flight[key].wait_recv()

    w_copies = [
        pltpu.make_async_copy(down_hbm, W.at[0], w_sem.at[0]),
        pltpu.make_async_copy(up_hbm, W.at[1], w_sem.at[1]),
    ]
    for copy in w_copies:
        copy.start()
    barrier = pltpu.get_barrier_semaphore()
    peers = local + zpeers + [xlo] + ypeers
    for peer in peers:
        pl.semaphore_signal(barrier, inc=1, device_id=peer, device_id_type=MESH)

    def block(a, zz, col):
        return G.at[a, zz // 2, zz % 2, col, c]

    def pair(a, zz):
        return G.at[a, zz // 2, zz % 2, :, c]

    def lane_col(lane):
        return xh if lane == 0 else 1 - xh

    def ring(a, lane, way, step, zz):
        ref = block(a, zz, lane_col(lane))
        send(("ring", a, lane, way, step), ref, ref, at(zoff(way), xh, c))

    def to_sibling(a, off):
        ref = pair(a, zoff(off))
        send(("sib", a, off % 8), ref, ref, sibling)

    def gather_start(a):
        ref = block(a, z, xh)
        send(("agx", a), ref, ref, xpart)
        for way in (1, -1):
            ring(a, 0, way, 1, z)

    def gather_other(a):
        arrived("agx", a)
        for way in (-1, 1):
            ring(a, 1, way, 1, z)
        to_sibling(a, 0)

    def gather_step(a, step):
        for lane in (0, 1):
            for way in (1, -1):
                if hops(lane, way) < step:
                    continue
                arrived("ring", a, lane, way, step)
                if step < hops(lane, way):
                    ring(a, lane, way, step + 1, zoff(-way * step))
        for way in (1, -1) if step < 4 else (1,):
            to_sibling(a, -way * step)

    def gather_end(a):
        for off in range(8):
            arrived("sib", a, off)

    def neighbour_rows(a):
        send(("xlo", a), G.at[a, :, 1 - xl, :, c], GP.at[a, :, :, c], xlo)

    def neighbour_share(a):
        arrived("xlo", a)
        ref = GP.at[a, :, :, c]
        send(("xlosib", a), ref, ref, sibling)

    def sums_local(phase):
        for j, peer in enumerate(local):
            send(("st", phase, j), ST.at[phase, 0], ST.at[phase, j + 1], peer)

    def sums_z(phase):
        for j in range(3):
            arrived("st", phase, j)
        SZ[phase, 0] = (ST[phase, 0] + ST[phase, 1]) + (ST[phase, 2] + ST[phase, 3])
        for j, peer in enumerate(zpeers):
            send(("sz", phase, j), SZ.at[phase, 0], SZ.at[phase, j + 1], peer)

    def sums_end(phase):
        for j in range(7):
            arrived("sz", phase, j)
        return jnp.sum(SZ[phase], axis=0)

    def turn(a):
        w_copies[a].wait()

        def body(i, carry):
            WT[a, i] = W[a, i].reshape(8 * rows, hidden).T
            return carry

        lax.fori_loop(0, 4, body, 0)

    def project(a):
        def body(i, total):
            return total + dot(WT[a, i], G[a, i].reshape(8 * rows, tokens))

        return lax.fori_loop(0, 4, body, jnp.zeros((hidden, tokens), F32))

    def partial(a, off, core):
        zz = zoff(off)
        return dot(W[a, zz // 2, zz % 2, :, core].reshape(2 * rows, hidden), AD[a]).reshape(
            2, rows, tokens
        )

    def scatter_sibling(a):
        for off in ORDER:
            VS[a, off % 8] = partial(a, off, 1 - c).astype(BF)
            send(("rsib", a, off % 8), VS.at[a, off % 8], R1.at[a, off % 8], sibling)

    def scatter_send(a, lane, way, step, value):
        w = (1 - way) // 2
        SB[a, lane, w, step - 1] = value.astype(BF)
        send(
            ("rring", a, lane, way, step),
            SB.at[a, lane, w, step - 1],
            RB.at[a, lane, w, step - 1],
            at(zoff(way), xh, c),
        )

    def scatter_own(a):
        for n, off in enumerate(ORDER):
            mine = partial(a, off, c)
            arrived("rsib", a, off % 8)
            PT[a, off % 8] = mine + R1[a, off % 8].astype(F32)
            if n == 2:
                for lane in (0, 1):
                    for way in (1, -1):
                        first = (way * hops(lane, way)) % 8
                        scatter_send(a, lane, way, 1, PT[a, first, lane_col(lane)])

    def received(a, lane, way, step):
        return RB[a, lane, (1 - way) // 2, step - 1].astype(F32)

    def scatter_step(a, step):
        for lane in (0, 1):
            for way in (1, -1):
                reach = hops(lane, way)
                if reach < step:
                    continue
                arrived("rring", a, lane, way, step)
                if step < reach:
                    off = (way * (reach - step)) % 8
                    value = received(a, lane, way, step) + PT[a, off, lane_col(lane)]
                    scatter_send(a, lane, way, step + 1, value)

    def scatter_total(a, lane):
        total = PT[a, 0, lane_col(lane)]
        for way in (1, -1):
            total = total + received(a, lane, way, hops(lane, way))
        return total

    def scatter_cross(a):
        XS[a] = scatter_total(a, 1).astype(BF)
        send(("rsx", a), XS.at[a], XR.at[a], xpart)

    def scatter_end(a):
        total = scatter_total(a, 0)
        arrived("rsx", a)
        return total + XR[a].astype(F32)

    grad_out = (gd_ref, gu_ref)

    def grad_block(a, j):
        yy = lax.rem(y + j, 4)
        mine = G[a, yy, xl].reshape(4 * rows, tokens)
        theirs = GP[a, yy].reshape(4 * rows, tokens)
        total = lax.dot_general(mine, AD[a], NT, preferred_element_type=F32)
        total = total + lax.dot_general(theirs, ADP[a], NT, preferred_element_type=F32)
        if j == 0:
            grad_out[a][...] = total
        else:
            GS[a, j - 1] = total.astype(BF)
            send(("grad", a, j), GS.at[a, j - 1], GR.at[a, j - 1], ypeers[j - 1])

    def grad_end(a):
        for j in (1, 3, 2):
            arrived("grad", a, j)
        grad_out[a][...] = (
            grad_out[a][...]
            + GR[a, 0].astype(F32)
            + GR[a, 1].astype(F32)
            + GR[a, 2].astype(F32)
        )

    x = x_ref[...].astype(F32)
    ST[0, 0, 0:1, :] = jnp.sum(x, axis=0, keepdims=True)
    ST[0, 0, 1:2, :] = jnp.sum(x * x, axis=0, keepdims=True)
    G[0, z // 2, z % 2, xh, c] = (cot_ref[...].astype(F32) * mod_ref[2]).astype(BF)
    pl.semaphore_wait(barrier, len(peers))
    sums_local(0)
    gather_start(0)
    turn(0)
    sums_z(0)
    gather_other(0)
    gather_step(0, 1)
    sums = sums_end(0)
    mean = sums[0:1, :] / width
    var = sums[1:2, :] / width - mean * mean
    rstd = lax.rsqrt(var + 1e-06)
    xhat = (x_ref[...].astype(F32) - mean) * rstd
    XH[...] = xhat
    G[1, z // 2, z % 2, xh, c] = (xhat * (1.0 + mod_ref[1]) + mod_ref[0]).astype(BF)
    gather_start(1)
    gather_step(0, 2)
    turn(1)
    gather_other(1)
    gather_step(0, 3)
    gather_step(1, 1)
    gather_step(0, 4)
    neighbour_rows(0)
    gather_step(1, 2)
    gather_end(0)
    DA[...] = project(0)
    gather_step(1, 3)
    neighbour_share(0)
    gather_step(1, 4)
    neighbour_rows(1)
    gather_end(1)
    pre = project(1)
    root = 0.7978845608028654
    bend = jnp.tanh(root * (pre + 0.044715 * (pre * pre * pre)))
    AD[0] = (0.5 * pre * (1.0 + bend)).astype(BF)
    send(("ad", 0), AD.at[0], ADP.at[0], xlo)
    slope = 0.5 * (1.0 + bend) + 0.5 * pre * (1.0 - bend * bend) * (
        root * (1.0 + 3.0 * 0.044715 * (pre * pre))
    )
    AD[1] = (DA[...] * slope).astype(BF)
    send(("ad", 1), AD.at[1], ADP.at[1], xlo)
    scatter_sibling(0)
    scatter_own(0)
    scatter_sibling(1)
    scatter_own(1)
    scatter_step(0, 1)
    neighbour_share(1)
    arrived("ad", 0)
    arrived("xlosib", 0)
    grad_block(0, 2)
    scatter_step(1, 1)
    grad_block(0, 1)
    scatter_step(0, 2)
    grad_block(0, 3)
    scatter_step(1, 2)
    arrived("ad", 1)
    arrived("xlosib", 1)
    grad_block(1, 2)
    scatter_step(0, 3)
    grad_block(1, 1)
    scatter_step(1, 3)
    grad_block(1, 3)
    scatter_step(0, 4)
    scatter_cross(0)
    scatter_step(1, 4)
    scatter_cross(1)
    grad_block(0, 0)
    grad_block(1, 0)
    dxhat = scatter_end(1) * (1.0 + mod_ref[1])
    ST[1, 0, 0:1, :] = jnp.sum(dxhat, axis=0, keepdims=True)
    ST[1, 0, 1:2, :] = jnp.sum(dxhat * XH[...], axis=0, keepdims=True)
    sums_local(1)
    velocity = scatter_end(0)
    mixed_ref[...] = (x_ref[...].astype(F32) + mod_ref[2] * velocity).astype(BF)
    sums_z(1)
    grad_end(0)
    sums = sums_end(1)
    tok_ref[...] = (
        cot_ref[...].astype(F32)
        + rstd * (dxhat - sums[0:1, :] / width - XH[...] * (sums[1:2, :] / width))
    ).astype(BF)
    grad_end(1)
    for copy in flight.values():
        copy.wait_send()


def lookup(modulation, buckets):
    n, kinds, cols = modulation.shape
    table = modulation.reshape(n, kinds * cols)
    high = lax.reduce_precision(table, 8, 7)
    rest = table - high
    middle = lax.reduce_precision(rest, 8, 7)
    low = rest - middle
    chosen = (lax.broadcasted_iota(jnp.int32, (n, buckets.shape[0]), 0) == buckets[None, :]).astype(BF)
    pieces = [
        lax.dot_general(
            piece.astype(BF), chosen, (((0,), (0,)), ((), ())), preferred_element_type=F32
        )
        for piece in (high, middle, low)
    ]
    return (pieces[0] + pieces[1] + pieces[2]).reshape(kinds, cols, buckets.shape[0])


def on_device(tokens, buckets, modulation, up_weight, down_weight, output_cotangent):
    batch, rows = tokens.shape
    hidden = up_weight.shape[1]
    groups = lax.axis_size("tensor")
    width = rows * groups
    shape5 = (4, 2, 2, 2, rows, hidden)
    cond = lookup(modulation, buckets)
    vmem = pl.BlockSpec(memory_space=pltpu.VMEM)
    anyspace = pl.BlockSpec(memory_space=pl.ANY)
    V = pltpu.VMEM
    mixed, tok, grad_down, grad_up = pl.pallas_call(
        functools.partial(block_kernel, width),
        out_shape=(
            jax.ShapeDtypeStruct((rows, batch), BF),
            jax.ShapeDtypeStruct((rows, batch), BF),
            jax.ShapeDtypeStruct((4 * rows, hidden), F32),
            jax.ShapeDtypeStruct((4 * rows, hidden), F32),
        ),
        in_specs=[vmem, vmem, vmem, anyspace, anyspace],
        out_specs=(vmem,) * 4,
        scratch_shapes=[
            V((2,) + shape5, BF),
            V((2, 4, hidden, 8 * rows), BF),
            V((2, 4, 2, 2, 2, rows, batch), BF),
            V((2, 4, 2, 2, rows, batch), BF),
            V((2, 4, 2, batch), F32),
            V((2, 8, 2, batch), F32),
            V((rows, batch), F32),
            V((hidden, batch), F32),
            V((2, hidden, batch), BF),
            V((2, hidden, batch), BF),
            V((2, 8, 2, rows, batch), BF),
            V((2, 8, 2, rows, batch), BF),
            V((2, 8, 2, rows, batch), F32),
            V((2, 2, 2, 4, rows, batch), BF),
            V((2, 2, 2, 4, rows, batch), BF),
            V((2, rows, batch), BF),
            V((2, rows, batch), BF),
            V((2, 3, 4 * rows, hidden), BF),
            V((2, 3, 4 * rows, hidden), BF),
            pltpu.SemaphoreType.DMA((N_COPIES,)),
            pltpu.SemaphoreType.DMA((N_COPIES,)),
            pltpu.SemaphoreType.DMA((2,)),
        ],
        compiler_params=pltpu.CompilerParams(
            collective_id=0, has_side_effects=True, vmem_limit_bytes=56 * 1024 * 1024
        ),
        name="mlp_block",
    )(
        tokens.T,
        output_cotangent.T,
        cond,
        down_weight.reshape(shape5),
        up_weight.reshape(shape5),
    )
    return mixed.T, tok.T, grad_up, grad_down


def solution(mesh):
    placed = (
        P("dp", "tensor"),
        P("dp"),
        P(None, None, "tensor"),
        P(None, "tensor"),
        P(None, "tensor"),
        P("dp", "tensor"),
    )
    return jax.shard_map(
        on_device,
        mesh=mesh,
        in_specs=placed,
        out_specs=(P("dp", "tensor"), P("dp", "tensor"), P("dp", "tensor"), P("dp", "tensor")),
        check_vma=False,
    )
```

```python
import functools

import jax
import jax.numpy as jnp
from jax import lax
from jax.experimental import pallas as pl
from jax.experimental.pallas import tpu as pltpu
from jax.sharding import PartitionSpec as P

MESH = pl.DeviceIdType.MESH
BF = jnp.bfloat16
F32 = jnp.float32
NT = (((1,), (1,)), ((), ()))
FIRST = (4, 3, -3)
REST = (2, -2, 1, -1, 0)
SENDS, RECEIVES = 75, 103


def hops(lane, way):
    return 4 if (lane == 0) == (way == 1) else 3


def dot(a, b):
    return jnp.dot(a, b, preferred_element_type=F32)


def block_kernel(
    width,
    x_hbm,
    cot_hbm,
    buckets_hbm,
    table_hbm,
    down_hbm,
    up_hbm,
    mixed_ref,
    tok_ref,
    gd_ref,
    gu_ref,
    x_ref,
    cot_ref,
    bucket_ref,
    table_ref,
    mod_ref,
    W,
    WT,
    G,
    GP,
    ST,
    SZ,
    SA,
    XH,
    DA,
    AD,
    ADP,
    VS,
    R1,
    PT,
    SB,
    RB,
    XS,
    XR,
    GS,
    GH,
    GR,
    send_sem,
    recv_sem,
    w_sem,
):
    d, t = lax.axis_index("dp"), lax.axis_index("tensor")
    z, xh, c = t // 4, (t // 2) % 2, t % 2
    y, xl = d // 2, d % 2
    rows, tokens = x_ref.shape
    hidden = W.shape[-1]

    def at(zz, hi, core):
        return (d, zz * 4 + hi * 2 + core)

    def zoff(off):
        return lax.rem(z + off % 8, 8)

    sibling = at(z, xh, 1 - c)
    xpart = at(z, 1 - xh, c)
    xcross = at(z, 1 - xh, 1 - c)
    zpeers = [at(zoff(k), xh, c) for k in range(1, 8)]
    xlo = (y * 2 + 1 - xl, t)
    ypeers = [(lax.rem(y + j, 4) * 2 + xl, t) for j in range(1, 4)]
    local = [sibling, xpart, xcross]

    flight, slots = {}, {}
    used = [0, 0]

    def make(src, dst, device, pair):
        return pltpu.make_async_remote_copy(
            src_ref=src,
            dst_ref=dst,
            send_sem=send_sem.at[pair[0]],
            recv_sem=recv_sem.at[pair[1]],
            device_id=device,
            device_id_type=MESH,
        )

    def new_pair(after=None):
        if after is None:
            first, used[0] = used[0], used[0] + 1
        else:
            flight.pop(after).wait_send()
            first = slots[after][0]
        used[1] += 1
        return first, used[1] - 1

    def send(key, src, dst, device, after=None):
        slots[key] = new_pair(after)
        flight[key] = make(src, dst, device, slots[key])
        flight[key].start()

    def send_in(group, total_src, total_dst, src, dst, device):
        if group not in slots:
            slots[group] = new_pair()
            flight[group] = make(total_src, total_dst, device, slots[group])
        make(src, dst, device, slots[group]).start()

    def arrived(*key):
        flight[key].wait_recv()

    barrier = pltpu.get_barrier_semaphore()
    peers = zpeers + local + [xlo] + ypeers
    for peer in peers:
        pl.semaphore_signal(barrier, inc=1, device_id=peer, device_id_type=MESH)
    in_copies = [
        pltpu.make_async_copy(src, dst, w_sem.at[n])
        for n, (src, dst) in enumerate(
            (
                (x_hbm, x_ref),
                (cot_hbm, cot_ref),
                (buckets_hbm, bucket_ref),
                (table_hbm, table_ref),
                (down_hbm, W.at[0]),
                (up_hbm, W.at[1]),
            )
        )
    ]
    for copy in in_copies:
        copy.start()

    def block(a, zz, col):
        return G.at[a, zz // 2, zz % 2, col, c]

    def pair(a, zz):
        return G.at[a, zz // 2, zz % 2, :, c]

    def lane_col(lane):
        return xh if lane == 0 else 1 - xh

    def ring(a, lane, way, step, zz):
        ref = block(a, zz, lane_col(lane))
        send(("ring", a, lane, way, step), ref, ref, at(zoff(way), xh, c))

    def to_sibling(a, off):
        ref = pair(a, zoff(off))
        send_in(
            ("sib", a), G.at[a, :, :, :, c], G.at[a, :, :, :, 1 - c], ref, ref, sibling
        )

    def gather_start(a):
        ref = block(a, z, xh)
        send(("agx", a), ref, ref, xpart)
        for way in (1, -1):
            ring(a, 0, way, 1, z)

    def gather_other(a):
        arrived("agx", a)
        for way in (-1, 1):
            ring(a, 1, way, 1, z)
        to_sibling(a, 0)

    def gather_step(a, lane, step):
        for way in (1, -1) if lane == 0 else (-1, 1):
            if hops(lane, way) < step:
                continue
            arrived("ring", a, lane, way, step)
            if step < hops(lane, way):
                ring(a, lane, way, step + 1, zoff(-way * step))
        if lane == 1:
            for way in (1, -1) if step < 4 else (1,):
                to_sibling(a, -way * step)

    def gather_end(a):
        arrived("sib", a)

    odd = lax.rem(z + 1 - xl, 2)
    far = (odd, 2 - 3 * odd, 5 * odd - 2, 4 - 7 * odd)

    def neighbour_rows(a, half):
        for n in (2 * half, 2 * half + 1):
            zz = lax.rem(z + far[n] + 8, 8)
            send_in(
                ("xlo", a),
                G.at[a, :, 1 - xl, :, c],
                GP.at[a, :, :, c],
                G.at[a, zz // 2, zz % 2, :, c],
                GP.at[a, zz // 2, :, c],
                xlo,
            )

    def neighbour_share(a):
        arrived("xlo", a)
        ref = GP.at[a, :, :, c]
        send(("xlosib", a), ref, ref, sibling)

    def sums_local():
        for j, peer in enumerate(local):
            send(("st", j), ST.at[0], ST.at[j + 1], peer)

    def sums_z():
        for j in range(3):
            arrived("st", j)
        SZ[0] = (ST[0] + ST[1]) + (ST[2] + ST[3])
        for j, peer in enumerate(zpeers):
            send(("sz", j), SZ.at[0], SZ.at[j + 1], peer)

    def sums_end():
        for j in range(7):
            arrived("sz", j)
        return jnp.sum(SZ[...], axis=0)

    def sums_all():
        for n in range(31, 0, -1):
            k, hi, core = n // 4, (n // 2) % 2, n % 2
            peer = at(zoff(k), xh if hi == 0 else 1 - xh, c if core == 0 else 1 - c)
            send_in(("sa",), SA.at[1:32], SA.at[1:32], SA.at[0], SA.at[n], peer)

    def sums_all_end():
        arrived("sa")
        return jnp.sum(SA[...], axis=0)

    def turn(a):
        in_copies[4 + a].wait()

        def body(i, carry):
            WT[a, i] = W[a, i].reshape(8 * rows, hidden).T
            return carry

        lax.fori_loop(0, 4, body, 0)

    def project(a):
        def body(i, total):
            return total + dot(WT[a, i], G[a, i].reshape(8 * rows, tokens))

        return lax.fori_loop(0, 4, body, jnp.zeros((hidden, tokens), F32))

    def partial(a, off, core):
        zz = zoff(off)
        return dot(W[a, zz // 2, zz % 2, :, core].reshape(2 * rows, hidden), AD[a]).reshape(
            2, rows, tokens
        )

    def scatter_sibling(a, offsets):
        for off in offsets:
            VS[a, off % 8] = partial(a, off, 1 - c).astype(BF)
            send(("rsib", a, off % 8), VS.at[a, off % 8], R1.at[a, off % 8], sibling)

    def scatter_send(a, lane, way, step, value):
        w = (1 - way) // 2
        SB[a, lane, w, step - 1] = value.astype(BF)
        send(
            ("rring", a, lane, way, step),
            SB.at[a, lane, w, step - 1],
            RB.at[a, lane, w, step - 1],
            at(zoff(way), xh, c),
            after=("ring", a, lane, way, step),
        )

    def scatter_own(a, offsets):
        for off in offsets:
            mine = partial(a, off, c)
            arrived("rsib", a, off % 8)
            PT[a, off % 8] = mine + R1[a, off % 8].astype(F32)

    def scatter_start(a):
        scatter_own(a, FIRST)
        for lane in (0, 1):
            for way in (1, -1):
                first = (way * hops(lane, way)) % 8
                scatter_send(a, lane, way, 1, PT[a, first, lane_col(lane)])

    def received(a, lane, way, step):
        return RB[a, lane, (1 - way) // 2, step - 1].astype(F32)

    def scatter_step(a, step):
        for lane in (0, 1):
            for way in (1, -1):
                reach = hops(lane, way)
                if reach < step:
                    continue
                arrived("rring", a, lane, way, step)
                if step < reach:
                    off = (way * (reach - step)) % 8
                    value = received(a, lane, way, step) + PT[a, off, lane_col(lane)]
                    scatter_send(a, lane, way, step + 1, value)

    def scatter_total(a, lane):
        total = PT[a, 0, lane_col(lane)]
        for way in (1, -1):
            total = total + received(a, lane, way, hops(lane, way))
        return total

    def scatter_cross(a):
        XS[a] = scatter_total(a, 1).astype(BF)
        send(("rsx", a), XS.at[a], XR.at[a], xpart)

    def scatter_end(a):
        total = scatter_total(a, 0)
        arrived("rsx", a)
        return total + XR[a].astype(F32)

    grad_out = (gd_ref, gu_ref)

    half = 2 * rows

    def grad_total(a, j):
        yy = lax.rem(y + j, 4)
        mine = G[a, yy, xl].reshape(4 * rows, tokens)
        theirs = GP[a, yy].reshape(4 * rows, tokens)
        total = lax.dot_general(mine, AD[a], NT, preferred_element_type=F32)
        return total + lax.dot_general(theirs, ADP[a], NT, preferred_element_type=F32)

    def grad_far(a):
        GS[a, 0] = grad_total(a, 2).astype(BF)
        for w, peer in enumerate((ypeers[0], ypeers[2])):
            part = GS.at[a, 0, w * half : (w + 1) * half]
            send(("far", a, w), part, GH.at[a, w], peer)

    def grad_near(a):
        total = grad_total(a, 1)
        arrived("far", a, 0)
        GS[a, 1, :half] = (total[:half] + GH[a, 0].astype(F32)).astype(BF)
        GS[a, 1, half:] = total[half:].astype(BF)
        send(("grad", a, 0), GS.at[a, 1], GR.at[a, 0], ypeers[0])
        total = grad_total(a, 3)
        arrived("far", a, 1)
        GS[a, 2, :half] = total[:half].astype(BF)
        GS[a, 2, half:] = (total[half:] + GH[a, 1].astype(F32)).astype(BF)
        send(("grad", a, 1), GS.at[a, 2], GR.at[a, 1], ypeers[2])

    def grad_own(a):
        grad_out[a][...] = grad_total(a, 0)

    def grad_end(a):
        for w in range(2):
            arrived("grad", a, w)
        grad_out[a][...] = grad_out[a][...] + GR[a, 0].astype(F32) + GR[a, 1].astype(F32)

    def lookup(kind, chosen):
        table = table_ref[kind]
        high = table.astype(BF)
        rest = table - high.astype(F32)
        middle = rest.astype(BF)
        low = (rest - middle.astype(F32)).astype(BF)
        mod_ref[kind] = (dot(high, chosen) + dot(middle, chosen)) + dot(low, chosen)

    def begin():
        for n in range(4):
            in_copies[n].wait()
        x = x_ref[...].astype(F32)
        ST[0, 0:1, :] = jnp.sum(x, axis=0, keepdims=True)
        ST[0, 1:2, :] = jnp.sum(x * x, axis=0, keepdims=True)
        here = lax.broadcasted_iota(jnp.int32, (table_ref.shape[2], tokens), 0)
        chosen = (here == bucket_ref[...]).astype(F32).astype(BF)
        lookup(2, chosen)
        G[0, z // 2, z % 2, xh, c] = (cot_ref[...].astype(F32) * mod_ref[2]).astype(BF)
        lookup(0, chosen)
        lookup(1, chosen)

    begin()
    pl.semaphore_wait(barrier, len(peers))
    sums_local()
    gather_start(0)
    turn(0)
    turn(1)
    gather_step(0, 0, 1)
    sums_z()
    gather_other(0)
    gather_step(0, 0, 2)
    gather_step(0, 1, 1)
    sums = sums_end()
    mean = sums[0:1, :] / width
    var = sums[1:2, :] / width - mean * mean
    rstd = lax.rsqrt(var + 1e-06)
    xhat = (x_ref[...].astype(F32) - mean) * rstd
    XH[...] = xhat
    G[1, z // 2, z % 2, xh, c] = (xhat * (1.0 + mod_ref[1]) + mod_ref[0]).astype(BF)
    gather_start(1)
    gather_step(0, 0, 3)
    gather_step(0, 1, 2)
    neighbour_rows(0, 0)
    gather_step(1, 0, 1)
    gather_step(0, 0, 4)
    gather_other(1)
    gather_step(0, 1, 3)
    gather_step(1, 0, 2)
    gather_step(1, 1, 1)
    gather_step(0, 1, 4)
    neighbour_rows(0, 1)
    gather_step(1, 0, 3)
    gather_step(1, 1, 2)
    neighbour_rows(1, 0)
    gather_end(0)
    DA[...] = project(0)
    gather_step(1, 0, 4)
    gather_step(1, 1, 3)
    neighbour_share(0)
    gather_step(1, 1, 4)
    gather_end(1)
    pre = project(1)
    root = 0.7978845608028654
    bend = jnp.tanh(root * (pre + 0.044715 * (pre * pre * pre)))
    AD[0] = (0.5 * pre * (1.0 + bend)).astype(BF)
    send(("ad", 0), AD.at[0], ADP.at[0], xlo)
    neighbour_rows(1, 1)
    slope = 0.5 * (1.0 + bend) + 0.5 * pre * (1.0 - bend * bend) * (
        root * (1.0 + 3.0 * 0.044715 * (pre * pre))
    )
    AD[1] = (DA[...] * slope).astype(BF)
    send(("ad", 1), AD.at[1], ADP.at[1], xlo)
    scatter_sibling(1, FIRST)
    scatter_sibling(1, REST)
    scatter_start(1)
    scatter_own(1, REST)
    scatter_sibling(0, FIRST)
    scatter_sibling(0, REST)
    scatter_step(1, 1)
    arrived("xlosib", 0)
    arrived("ad", 0)
    grad_far(0)
    scatter_start(0)
    scatter_step(1, 2)
    scatter_own(0, REST)
    scatter_step(0, 1)
    grad_near(0)
    scatter_step(1, 3)
    neighbour_share(1)
    scatter_step(0, 2)
    arrived("ad", 1)
    arrived("xlosib", 1)
    grad_far(1)
    scatter_step(1, 4)
    scatter_cross(1)
    scatter_step(0, 3)
    grad_own(0)
    grad_own(1)
    dxhat = scatter_end(1) * (1.0 + mod_ref[1])
    SA[0, 0:1, :] = jnp.sum(dxhat, axis=0, keepdims=True)
    SA[0, 1:2, :] = jnp.sum(dxhat * XH[...], axis=0, keepdims=True)
    sums_all()
    grad_near(1)
    scatter_step(0, 4)
    scatter_cross(0)
    velocity = scatter_end(0)
    mixed_ref[...] = (x_ref[...].astype(F32) + mod_ref[2] * velocity).astype(BF)
    grad_end(0)
    sums = sums_all_end()
    tok_ref[...] = (
        cot_ref[...].astype(F32)
        + rstd * (dxhat - sums[0:1, :] / width - XH[...] * (sums[1:2, :] / width))
    ).astype(BF)
    grad_end(1)

    def finish():
        for copy in flight.values():
            copy.wait_send()

    finish()
    assert used == [SENDS, RECEIVES], used


def on_device(tokens, buckets, modulation, up_weight, down_weight, output_cotangent):
    batch, rows = tokens.shape
    hidden = up_weight.shape[1]
    groups = lax.axis_size("tensor")
    width = rows * groups
    shape5 = (4, 2, 2, 2, rows, hidden)
    table = jnp.transpose(modulation, (1, 2, 0))
    vmem = pl.BlockSpec(memory_space=pltpu.VMEM)
    hbm = pl.BlockSpec(memory_space=pltpu.HBM)
    V = pltpu.VMEM
    mixed, tok, grad_down, grad_up = pl.pallas_call(
        functools.partial(block_kernel, width),
        out_shape=(
            V((rows, batch), BF),
            V((rows, batch), BF),
            V((4 * rows, hidden), F32),
            V((4 * rows, hidden), F32),
        ),
        in_specs=[hbm] * 6,
        out_specs=(vmem,) * 4,
        scratch_shapes=[
            V((rows, batch), BF),
            V((rows, batch), BF),
            V((1, batch), jnp.int32),
            V(table.shape, F32),
            V((3, rows, batch), F32),
            V((2,) + shape5, BF),
            V((2, 4, hidden, 8 * rows), BF),
            V((2, 4, 2, 2, 2, rows, batch), BF),
            V((2, 4, 2, 2, rows, batch), BF),
            V((4, 2, batch), F32),
            V((8, 2, batch), F32),
            V((32, 2, batch), F32),
            V((rows, batch), F32),
            V((hidden, batch), F32),
            V((2, hidden, batch), BF),
            V((2, hidden, batch), BF),
            V((2, 8, 2, rows, batch), BF),
            V((2, 8, 2, rows, batch), BF),
            V((2, 8, 2, rows, batch), F32),
            V((2, 2, 2, 4, rows, batch), BF),
            V((2, 2, 2, 4, rows, batch), BF),
            V((2, rows, batch), BF),
            V((2, rows, batch), BF),
            V((2, 3, 4 * rows, hidden), BF),
            V((2, 2, 2 * rows, hidden), BF),
            V((2, 2, 4 * rows, hidden), BF),
            pltpu.SemaphoreType.DMA((SENDS,)),
            pltpu.SemaphoreType.DMA((RECEIVES,)),
            pltpu.SemaphoreType.DMA((6,)),
        ],
        compiler_params=pltpu.CompilerParams(
            collective_id=0, has_side_effects=True, vmem_limit_bytes=36 * 1024 * 1024
        ),
        name="mlp_block",
    )(
        *(
            pltpu.with_memory_space_constraint(v, pltpu.HBM)
            for v in (
                tokens.T,
                output_cotangent.T,
                buckets.reshape(1, batch),
                table,
                down_weight.reshape(shape5),
                up_weight.reshape(shape5),
            )
        )
    )
    return mixed.T, tok.T, grad_up, grad_down


def solution(mesh):
    placed = (
        P("dp", "tensor"),
        P("dp"),
        P(None, None, "tensor"),
        P(None, "tensor"),
        P(None, "tensor"),
        P("dp", "tensor"),
    )
    return jax.shard_map(
        on_device,
        mesh=mesh,
        in_specs=placed,
        out_specs=(P("dp", "tensor"), P("dp", "tensor"), P("dp", "tensor"), P("dp", "tensor")),
        check_vma=False,
    )
```
